32 devices in a mesh: grp: 8 (over z, x), tp: 4 (over y, core).
Axes of the slice: x: 2, y: 2, z: 4, core: 2. Of those that a mesh axis runs over, the one named last changes fastest.
Arguments:
- activations: bfloat16 [192, 5120], P('grp', 'tp'), may hold values from -6 to 6
- upstream: bfloat16 [384, 1024], P('grp', 'tp'), may hold values from -22 to 22, as said below
- row_lengths: int32 [8, 8], P('grp'), may hold values from 1 to 6, 24 in all within a row
- learner_of: int32 [8, 8], P('grp'), may hold values from 0 to 7, each once within a row
- rewards: float32 [8, 8], P('grp'), may hold values from -10.5 to 10.5
- prompt_group: int32 [8, 8], P('grp'), may hold values from 0 to 31
Outputs:
- gradient: float32 [5120, 1024], P('tp')
- ghost: float32 [8, 8], P('grp')
The draws below stay inside these ranges and needn't reach their ends.
Inputs may be any that keep to these rules, and one draw needn't show every extreme that they name: `row_lengths`: each row lists the token counts of the finished rows of one index of grp in packing order; they sum to 24 and the largest is exactly 6, so at most 6 tokens go from one source to one learner shard, reached by every source. `learner_of`: each row is a permutation: every source sends exactly one finished row to every learner shard. `upstream`: slot rows at or past the length of their finished row are not read.
All inputs are finite; a program needn't handle non-finite values.
Results may differ from the reference program's by a relative error of at most 0.0042.
Values may be sent and summed in bfloat16 or wider, within the bound.
No kernel may reach another device: no remote copies, remote signals or barrier semaphores. Data moves between devices by JAX's collectives and lax.ppermute only.
A program may use at most 64 MiB of HBM per device.

```python
import math
import jax
import jax.numpy as jnp
import numpy as np
from jax import lax

D = 5120
VW = 1024
LMAX = 6
NSEQ = 8
SLOTS = 48
TOK_DEV = 24
TOKENS = 192
GROUPS = 32
N_GRP = 8


def draw_upstream(key, part):
    key_noise, key_column, key_row = jax.random.split(key, 3)
    total_rows = SLOTS * N_GRP
    column_scale = 10.0 ** (jax.random.uniform(key_column, (1, VW), dtype=jnp.float32) - 0.5)
    row_scale = 3.0 ** (jax.random.uniform(key_row, (total_rows, 1), dtype=jnp.float32) - 0.5)
    values = jnp.clip(jax.random.normal(key_noise, (total_rows, VW), dtype=jnp.float32), -4.0, 4.0)
    return (values * column_scale * row_scale).astype(jnp.bfloat16)


def draw_rewards(key, part):
    source_scale = 1.0 + 2.0 * jnp.arange(N_GRP, dtype=jnp.float32)[:, None] / (N_GRP - 1)
    values = jnp.clip(jax.random.normal(key, (N_GRP, NSEQ), dtype=jnp.float32), -3.5, 3.5)
    return (values * source_scale).astype(jnp.float32)


def with_ends(array, stream_key, least, top_value):
    place = [jax.random.randint(jax.random.fold_in(stream_key, axis), (), 0, length) for axis, length in enumerate(array.shape)]
    longest = array.shape.index(max(array.shape))
    neighbour = place[:longest] + [(place[longest] + 1) % array.shape[longest]] + place[longest + 1:]
    return array.at[tuple(place)].set(least).at[tuple(neighbour)].set(top_value)


def levels(stream_key, dims, pieces, low, high):
    loudness = 1.0
    for dim, parts in pieces:
        draws = jax.random.uniform(jax.random.fold_in(jax.random.fold_in(stream_key, 6), dim), (parts,), jnp.float32, low / len(pieces), high / len(pieces))
        loudness = loudness * jnp.repeat(jnp.exp(draws), dims[dim] // parts).reshape((-1,) + (1,) * (len(dims) - 1 - dim))
    return loudness


def length_profile(amount, total, bound, lean):
    portions = [(1 << 20) // math.isqrt(standing ** lean) + 1 for standing in range(2, amount + 1)]
    spare, holding = total - bound - (amount - 1), [1] * (amount - 1)
    while spare > 0:
        candidates = [i for i in range(amount - 1) if holding[i] < bound]
        pool, left = sum([portions[i] for i in candidates]), spare
        for i in candidates:
            addition = min(bound - holding[i], max(1, left * portions[i] // pool), spare)
            holding[i] = holding[i] + addition
            spare = spare - addition
    return np.array([bound] + holding)


def ragged(stream_key, amount, total, reach, slope):
    if amount == 2:
        one = jax.random.randint(stream_key, (), max(1, total - reach), min(reach, total - 1) + 1)
        return jnp.stack([one, total - one])
    lengths = jnp.asarray(length_profile(amount, total, reach, slope), jnp.int32)
    pairs = (amount - 1) // 2
    source_of, sink = lengths[1:1 + 2 * pairs:2], lengths[2:2 + 2 * pairs:2]
    slack = jnp.minimum(source_of - 1, reach - sink)
    moved = jax.random.randint(jax.random.fold_in(stream_key, 1), (pairs,), 0, 1 << 20) % (slack + 1)
    lengths = lengths.at[1:1 + 2 * pairs:2].set(source_of - moved).at[2:2 + 2 * pairs:2].set(sink + moved)
    return lengths[jax.random.permutation(jax.random.fold_in(stream_key, 2), amount)]


def centred(stream_key, dims, scale, reach, cuts=(), kind=jnp.bfloat16):
    level = levels(stream_key, dims, cuts, -0.22, 0.18) if cuts else 1.0
    values = jax.random.normal(stream_key, dims, jnp.float32) * scale * level
    return jnp.minimum(jnp.maximum(values, -reach), reach).astype(kind)


def setup_inputs(seed: int = 0) -> dict:
    key_list = jax.random.split(jax.random.key(seed), 7)
    return {
        "activations": centred(key_list[0], (TOKENS, D), 1.0, 6.0, ((0, 8), (1, 4))),
        "upstream": draw_upstream(jax.random.fold_in(key_list[6], 71), 0),
        "row_lengths": jax.vmap(lambda own: ragged(own, NSEQ, TOK_DEV, LMAX, 2))(jax.random.split(key_list[2], N_GRP)).reshape((N_GRP, NSEQ)).astype(jnp.int32),
        "learner_of": jax.vmap(lambda own: jax.random.permutation(own, N_GRP))(jax.random.split(key_list[3], N_GRP)).reshape((N_GRP, NSEQ)).astype(jnp.int32),
        "rewards": draw_rewards(jax.random.fold_in(key_list[6], 71), 0),
        "prompt_group": with_ends(jax.random.randint(key_list[5], (N_GRP, NSEQ), 0, GROUPS), jax.random.fold_in(key_list[5], 1), 0, GROUPS - 1).astype(jnp.int32),
    }


epsilon = 1e-06
clip_limit = 3.0

def reference(activations, upstream, row_lengths, learner_of, rewards, prompt_group):
    flat_reward = rewards.reshape(-1)
    flat_group = prompt_group.reshape(-1).astype(jnp.int32)
    group_total = jax.ops.segment_sum(flat_reward, flat_group, num_segments=GROUPS)
    group_count = jax.ops.segment_sum(jnp.ones_like(flat_reward), flat_group, num_segments=GROUPS)
    group_mean = group_total / jnp.maximum(group_count, 1.0)
    advantage = flat_reward - group_mean[flat_group]
    coef = advantage / (group_count[flat_group] * row_lengths.reshape(-1).astype(jnp.float32))
    coef = coef.astype(jnp.bfloat16).reshape(N_GRP, NSEQ)
    starts = (jnp.cumsum(row_lengths, axis=1) - row_lengths).astype(jnp.int32)
    position = jnp.arange(LMAX, dtype=jnp.int32)

    def one_source(running, source):
        gradient, ghost = running
        start_row = starts[source]
        seq_len = row_lengths[source]
        target = learner_of[source].astype(jnp.int32)
        is_valid = position[None, :] < seq_len[:, None]
        token_index = (source * TOK_DEV + start_row[:, None] + position[None, :]).astype(jnp.int32)
        token_index = jnp.where(is_valid, token_index, 0).astype(jnp.int32)
        slot_index = ((target[:, None] * N_GRP + source) * LMAX + position[None, :]).astype(jnp.int32)
        rows_x = jnp.where(is_valid[..., None], activations[token_index], jnp.zeros((), jnp.bfloat16))
        rows_u = jnp.where(is_valid[..., None], upstream[slot_index], jnp.zeros((), jnp.bfloat16))
        float_x = rows_x.astype(jnp.float32)
        float_u = rows_u.astype(jnp.float32)
        gram_x = jnp.einsum('str,sur->stu', float_x, float_x)
        gram_u = jnp.einsum('str,sur->stu', float_u, float_u)
        squares = lax.optimization_barrier(jnp.sum(gram_x * gram_u, axis=(1, 2)))
        ghost_rms = jnp.sqrt(squares / (D * VW) + epsilon)
        clip_factor = clip_limit / jnp.maximum(ghost_rms, clip_limit)
        factor = coef[source].astype(jnp.float32) * clip_factor
        scaled = (float_u * factor[:, None, None]).astype(jnp.bfloat16)
        partial_grad = jnp.dot(rows_x.reshape(-1, D).T, scaled.reshape(-1, VW), preferred_element_type=jnp.float32)
        ghost = ghost.at[target, source].set(ghost_rms)
        return ((gradient + partial_grad, ghost), None)
    initial = (jnp.zeros((D, VW), jnp.float32), jnp.zeros((N_GRP, NSEQ), jnp.float32))
    final, unused = lax.scan(one_source, initial, jnp.arange(N_GRP, dtype=jnp.int32))
    return (final[0], final[1])
```

```python
import functools

import jax
import jax.numpy as jnp
from jax import lax
from jax.experimental import pallas as pl
from jax.experimental.pallas import tpu as pltpu
from jax.sharding import PartitionSpec as P

D = 5120
PGRP = 4
VW = 1024
LMAX = 6
HALF = 64
LANES = 128
SUB = 8
TILE = 16

epsilon = 1e-06
clip_limit = 3.0


def token_gram(flat):
    return lax.dot_general(flat, flat, (((1,), (1,)), ((), ())), preferred_element_type=jnp.float32)


def row_squares(left, right, row_slots):
    flat_left = left.reshape(-1, left.shape[2])
    flat_right = right.reshape(-1, right.shape[2])
    gram_left = token_gram(flat_left)
    gram_right = token_gram(flat_right)
    owner = jnp.arange(flat_left.shape[0], dtype=jnp.int32) // row_slots
    same_row = owner[:, None] == owner[None, :]
    per_token = jnp.sum(jnp.where(same_row, gram_left * gram_right, 0.0), axis=1)
    return jnp.sum(per_token.reshape(-1, row_slots), axis=1)


def general(activations, upstream, row_lengths, learner_of, rewards, prompt_group):
    sources = lax.axis_size("grp")
    group_number = PGRP * sources
    seq_len = row_lengths[0]
    targets = learner_of[0]
    reward = rewards[0]
    labels = prompt_group[0]
    member = (labels[:, None] == jnp.arange(group_number, dtype=jnp.int32)[None, :]).astype(
        jnp.float32
    )
    local_total = jnp.dot(reward, member, precision=lax.Precision.HIGHEST)
    local_count = jnp.sum(member, axis=0)
    group_total, group_count = lax.psum((local_total, local_count), "grp")
    group_mean = group_total / jnp.maximum(group_count, 1.0)
    advantage = reward - jnp.dot(member, group_mean, precision=lax.Precision.HIGHEST)
    members = jnp.dot(member, group_count, precision=lax.Precision.HIGHEST)
    weight = advantage / (members * seq_len.astype(jnp.float32))
    starts = jnp.cumsum(seq_len) - seq_len
    to_learner = targets[None, :] == jnp.arange(sources, dtype=jnp.int32)[:, None]
    slot_len = jnp.sum(jnp.where(to_learner, seq_len[None, :], 0), axis=1)
    slot_start = jnp.sum(jnp.where(to_learner, starts[None, :], 0), axis=1)
    slot_coef = jnp.sum(jnp.where(to_learner, weight[None, :], 0.0), axis=1).astype(jnp.bfloat16)
    position = jnp.arange(LMAX, dtype=jnp.int32)
    is_valid = position[None, :] < slot_len[:, None]
    token_index = jnp.where(is_valid, slot_start[:, None] + position[None, :], 0)
    send_x = jnp.where(is_valid[..., None], activations[token_index], jnp.zeros((), jnp.bfloat16))
    slot_upstream = upstream.reshape(sources, LMAX, upstream.shape[1])
    rows_x, row_coef = (
        lax.all_to_all(send_x, "grp", split_axis=0, concat_axis=0, tiled=True),
        lax.all_to_all(slot_coef, "grp", split_axis=0, concat_axis=0, tiled=True),
    )
    gathered = lax.all_gather(slot_upstream, "tp", axis=2, tiled=True)
    partial_value = row_squares(rows_x, gathered, LMAX)
    squares = lax.psum(partial_value, "tp")
    ghost_rms = jnp.sqrt(squares / (D * VW) + epsilon)
    clip_factor = clip_limit / jnp.maximum(ghost_rms, clip_limit)
    factor = row_coef.astype(jnp.float32) * clip_factor
    scaled = (gathered.astype(jnp.float32) * factor[:, None, None]).astype(jnp.bfloat16)
    local_term = lax.dot_general(
        rows_x.reshape(-1, rows_x.shape[2]),
        scaled.reshape(-1, scaled.shape[2]),
        (((0,), (0,)), ((), ())),
        preferred_element_type=jnp.float32,
    )
    gradient = lax.psum(local_term, "grp")
    return (gradient, ghost_rms[None, :])


def iota(shape, axis):
    return lax.broadcasted_iota(jnp.int32, shape, axis)


def terms(value):
    high = value.astype(jnp.bfloat16)
    rest = value - high.astype(jnp.float32)
    middle = rest.astype(jnp.bfloat16)
    low = (rest - middle.astype(jnp.float32)).astype(jnp.bfloat16)
    return high, middle, low


def mm(left, right, dims=((1,), (0,))):
    return lax.dot_general(left, right, (dims, ((), ())), preferred_element_type=jnp.float32)


NT = ((1,), (1,))
TN = ((0,), (0,))


def onehot(condition):
    return jnp.where(condition, 1.0, 0.0).astype(jnp.bfloat16)


def pack_kernel(row_max, len_ref, learner_ref, reward_ref, group_ref, x_ref, u_ref, out_ref):
    tokens, features = x_ref.shape
    slots, width = u_ref.shape
    rows = len_ref.shape[1]
    lane = iota((SUB, LANES), 1)
    row_of = lax.div(lane, row_max)
    place = lane - row_of * row_max
    table_len = jnp.zeros((SUB, LANES), jnp.int32)
    table_start = jnp.zeros((SUB, LANES), jnp.int32)
    table_group = jnp.zeros((SUB, LANES), jnp.int32)
    table_reward = jnp.zeros((SUB, LANES), jnp.float32)
    start = jnp.int32(0)
    for k in range(rows):
        mine = row_of == learner_ref[0, k]
        table_len = jnp.where(mine, len_ref[0, k], table_len)
        table_start = jnp.where(mine, start, table_start)
        table_group = jnp.where(mine, group_ref[0, k], table_group)
        table_reward = jnp.where(mine, reward_ref[0, k], table_reward)
        start = start + len_ref[0, k]
    source_token = jnp.where(place < table_len, table_start + place, -1)
    token_at = onehot(iota((tokens, LANES), 0) == source_token[:1])
    x = x_ref[...]
    u = u_ref[...]
    slot_x = mm(token_at, x, TN).astype(jnp.bfloat16)
    slot_u = mm(onehot(iota((LANES, slots), 0) == iota((LANES, slots), 1) + HALF), u).astype(jnp.bfloat16)
    gram = mm(slot_x, slot_x, NT) + mm(slot_u, slot_u, NT)
    across, down = iota((LANES, LANES), 1), iota((LANES, LANES), 0)
    half_across, half_down = lax.div(across, HALF), lax.div(down, HALF)
    local_across, local_down = across - half_across * HALF, down - half_down * HALF
    same = (half_across == half_down) & (lax.div(local_across, row_max) == lax.div(local_down, row_max))
    gram = jnp.where(same, gram, 0.0)
    token_across = iota((SUB, LANES), 1)
    token_across = token_across - lax.div(token_across, HALF) * HALF
    pick = onehot(lax.rem(token_across, row_max) == iota((SUB, LANES), 0))
    gram_terms = [mm(pick, term) for term in terms(gram)]
    reward_terms = [term.astype(jnp.float32) for term in terms(table_reward)]
    group_high = lax.div(table_group, 256)
    values = reward_terms + [
        v.astype(jnp.float32) for v in (group_high, table_group - group_high * 256, table_len, table_start)
    ]
    which = iota((SUB, LANES), 0)
    table = jnp.zeros((SUB, LANES), jnp.float32)
    for index, value in enumerate(values):
        table = jnp.where(which == index, value, table)
    small = jnp.concatenate(
        [
            jnp.concatenate([gram_terms[0], gram_terms[1]], axis=1),
            jnp.concatenate([gram_terms[2], table], axis=1),
        ],
        axis=0,
    ).astype(jnp.bfloat16)
    out_ref[:slots] = u
    out_ref[slots : slots + TILE] = small
    base = slots + TILE
    for chunk in range(features // width):
        out_ref[base + chunk * tokens : base + (chunk + 1) * tokens] = x[:, chunk * width : (chunk + 1) * width]


def final_kernel(sources, parts, row_max, total, *refs):
    blocks = refs[:sources]
    heads = refs[sources : sources + parts]
    grad_ref, ghost_ref, u_ref = refs[sources + parts :]
    me = lax.axis_index("grp")
    my_part = lax.axis_index("tp")
    head = HALF
    width = heads[0].shape[1]
    slots = sources * HALF
    tokens = u_ref.shape[0] // sources
    depth = sources * LANES

    lane = iota((1, slots), 1)
    learner = lax.bitwise_xor(lax.div(lane, HALF), me)
    within = lane - lax.div(lane, HALF) * HALF
    source = lax.div(within, row_max)
    place = within - source * row_max
    used = source < sources

    down = iota((depth, slots), 0)
    origin = lax.bitwise_xor(lax.div(down, LANES), me)
    local = down - lax.div(down, LANES) * LANES
    spread_x = onehot((local == learner * row_max + place) & (origin == source) & used)
    spread_u = onehot((local == within + HALF) & (origin == learner) & used)

    sum_x = jnp.zeros((SUB, slots), jnp.float32)
    sum_u = jnp.zeros((SUB, slots), jnp.float32)
    table = None
    for q in range(parts):
        small = [heads[q][m * head + head - TILE : (m + 1) * head, :].astype(jnp.float32) for m in range(sources)]
        first = jnp.concatenate([s[:SUB, :LANES] for s in small], axis=1)
        second = jnp.concatenate([s[:SUB, LANES:] for s in small], axis=1)
        third = jnp.concatenate([s[SUB:, :LANES] for s in small], axis=1)
        stack = [first, second, third]
        if q == 0:
            stack.append(jnp.concatenate([s[SUB:, LANES:] for s in small], axis=1))
        stack = jnp.concatenate(stack, axis=0).astype(jnp.bfloat16)
        by_x = mm(stack, spread_x)
        by_u = mm(stack[: 3 * SUB], spread_u)
        if q == 0:
            table = by_x[3 * SUB :]
        sum_x += by_x[:SUB] + by_x[SUB : 2 * SUB] + by_x[2 * SUB : 3 * SUB]
        sum_u += by_u[:SUB] + by_u[SUB : 2 * SUB] + by_u[2 * SUB :]

    per_slot = jnp.sum(sum_x * sum_u, axis=0, keepdims=True)
    across, rows = iota((slots, slots), 1), iota((slots, slots), 0)
    half_a, half_r = lax.div(across, HALF), lax.div(rows, HALF)
    same_row = onehot(
        (half_a == half_r) & (lax.div(across - half_a * HALF, row_max) == lax.div(rows - half_r * HALF, row_max))
    )
    slot_terms = jnp.concatenate(
        [term.astype(jnp.float32) for term in terms(per_slot)] + [jnp.zeros((SUB - 3, slots), jnp.float32)], axis=0
    ).astype(jnp.bfloat16)
    squares = mm(slot_terms, same_row)
    squares = squares[0:1] + squares[1:2] + squares[2:3]
    ghost = jnp.sqrt(squares / total + epsilon)
    clip = clip_limit / jnp.maximum(ghost, clip_limit)

    reward = table[0:1] + table[1:2] + table[2:3]
    group = table[3:4] * 256.0 + table[4:5]
    length, begin = table[5:6], table[6:7]
    group_column = jnp.transpose(jnp.concatenate([group] * SUB, axis=0))[:, :1]
    together = onehot(group_column == group)
    one_per_row = (place == 0) & used
    counted = jnp.concatenate([table[0:3], jnp.ones((1, slots), jnp.float32)] * 2, axis=0)
    counted = jnp.where(one_per_row, counted, 0.0).astype(jnp.bfloat16)
    sums = mm(counted, together)
    group_total = sums[0:1] + sums[1:2] + sums[2:3]
    count = sums[3:4]
    advantage = reward - group_total / jnp.maximum(count, 1.0)
    coef = advantage / (count * jnp.maximum(length, 1.0))
    coef = coef.astype(jnp.bfloat16).astype(jnp.float32)
    factor = coef * clip

    row = iota((sources * tokens, slots), 0)
    token_source = lax.bitwise_xor(lax.div(row, tokens), me)
    token = row - lax.div(row, tokens) * tokens
    valid = used & (place.astype(jnp.float32) < length)
    target = jnp.where(valid, begin.astype(jnp.int32) + place, -1)
    chosen = (token == target) & (token_source == source)
    factor_high = factor.astype(jnp.bfloat16)
    factor_low = (factor - factor_high.astype(jnp.float32)).astype(jnp.bfloat16)
    pick_high = jnp.where(chosen, factor_high.astype(jnp.float32), 0.0).astype(jnp.bfloat16)
    pick_low = jnp.where(chosen, factor_low.astype(jnp.float32), 0.0).astype(jnp.bfloat16)
    for q in range(parts):
        columns = heads[q][...]
        scaled = (mm(pick_high, columns) + mm(pick_low, columns)).astype(jnp.bfloat16)
        at = pl.multiple_of(lax.bitwise_xor(my_part, q) * width, width)
        u_ref[:, pl.ds(at, width)] = scaled
    scaled = u_ref[...]
    for chunk in range(grad_ref.shape[0] // width):
        base = head + chunk * tokens
        x = jnp.concatenate([b[base : base + tokens, :] for b in blocks], axis=0)
        grad_ref[chunk * width : (chunk + 1) * width, :] = mm(x, scaled, TN)

    out_lane = iota((LANES, LANES), 1)
    ghost_pick = jnp.where(iota((LANES, LANES), 0) == out_lane * row_max, 1.0, 0.0)
    own = jnp.concatenate([ghost[:, :LANES]] * SUB, axis=0)
    own = lax.dot_general(
        own, ghost_pick, (((1,), (0,)), ((), ())), precision=lax.Precision.HIGHEST, preferred_element_type=jnp.float32
    )
    ghost_ref[...] = own[:1, :sources]


def swap(value, axis, mask):
    size = lax.axis_size(axis)
    return lax.ppermute(value, axis, [(i, i ^ mask) for i in range(size)])


def gathered(activations, upstream, row_lengths, learner_of, rewards, prompt_group):
    sources = lax.axis_size("grp")
    parts = lax.axis_size("tp")
    tokens, features = activations.shape
    slots, width = upstream.shape
    row_max = slots // sources
    vmem = pl.BlockSpec(memory_space=pltpu.VMEM)
    smem = pl.BlockSpec(memory_space=pltpu.SMEM)
    packed_rows = HALF + features // width * tokens
    packed = pl.pallas_call(
        functools.partial(pack_kernel, row_max),
        out_shape=jax.ShapeDtypeStruct((packed_rows, width), jnp.bfloat16),
        in_specs=[smem] * 4 + [vmem] * 2,
        out_specs=vmem,
        name="pack",
    )(row_lengths, learner_of, rewards, prompt_group, activations, upstream)
    blocks = {0: packed}
    masks = [m for m in range(sources - 2, 0, -2)]
    for m in masks:
        blocks[m] = swap(packed, "grp", m)
    for m in [0] + masks[::-1]:
        blocks[m + 1] = swap(blocks[m], "grp", 1)
    ordered = [blocks[m] for m in range(sources)]
    heads = [jnp.concatenate([b[:HALF] for b in ordered], axis=0)]
    bit = parts // 2
    order = [0]
    while bit:
        heads = heads + [swap(h, "tp", bit) for h in heads]
        order = order + [o ^ bit for o in order]
        bit //= 2
    heads = [heads[order.index(q)] for q in range(parts)]
    gradient, ghost = pl.pallas_call(
        functools.partial(final_kernel, sources, parts, row_max, float(features * parts * width * parts)),
        out_shape=(
            jax.ShapeDtypeStruct((features, width * parts), jnp.float32),
            jax.ShapeDtypeStruct((1, sources), jnp.float32),
        ),
        in_specs=[vmem] * (sources + parts),
        out_specs=(vmem, vmem),
        scratch_shapes=[pltpu.VMEM((sources * tokens, width * parts), jnp.bfloat16)],
        compiler_params=pltpu.CompilerParams(vmem_limit_bytes=60000 * 1024),
        name="final",
    )(*ordered, *heads)
    return gradient, ghost


def power_of_two(value):
    return value & (value - 1) == 0


def local(activations, upstream, *table):
    sources = lax.axis_size("grp")
    parts = lax.axis_size("tp")
    tokens, features = activations.shape
    slots, width = upstream.shape
    fits = (
        power_of_two(sources)
        and power_of_two(parts)
        and slots == HALF - TILE
        and sources <= SUB
        and width == 2 * LANES
        and features % width == 0
        and tokens % SUB == 0
    )
    return (gathered if fits else general)(activations, upstream, *table)


def solution(mesh):
    in_specs = (
        P("grp", "tp"),
        P("grp", "tp"),
        P("grp", None),
        P("grp", None),
        P("grp", None),
        P("grp", None),
    )
    out_specs = (P("tp", None), P("grp", None))
    return jax.shard_map(local, mesh=mesh, in_specs=in_specs, out_specs=out_specs, check_vma=False)
```

```python
import functools

import jax
import jax.numpy as jnp
from jax import lax
from jax.experimental import pallas as pl
from jax.experimental.pallas import tpu as pltpu
from jax.sharding import PartitionSpec as P

D = 5120
PGRP = 4
VW = 1024
LMAX = 6
HALF = 64
LANES = 128
SUB = 8
TILE = 16
MIB = 1 << 20

epsilon = 1e-06
clip_limit = 3.0


def token_gram(flat):
    return lax.dot_general(flat, flat, (((1,), (1,)), ((), ())), preferred_element_type=jnp.float32)


def row_squares(left, right, row_slots):
    flat_left = left.reshape(-1, left.shape[2])
    flat_right = right.reshape(-1, right.shape[2])
    gram_left = token_gram(flat_left)
    gram_right = token_gram(flat_right)
    owner = jnp.arange(flat_left.shape[0], dtype=jnp.int32) // row_slots
    same_row = owner[:, None] == owner[None, :]
    per_token = jnp.sum(jnp.where(same_row, gram_left * gram_right, 0.0), axis=1)
    return jnp.sum(per_token.reshape(-1, row_slots), axis=1)


def general(activations, upstream, row_lengths, learner_of, rewards, prompt_group):
    sources = lax.axis_size("grp")
    group_number = PGRP * sources
    seq_len = row_lengths[0]
    targets = learner_of[0]
    reward = rewards[0]
    labels = prompt_group[0]
    member = (labels[:, None] == jnp.arange(group_number, dtype=jnp.int32)[None, :]).astype(
        jnp.float32
    )
    local_total = jnp.dot(reward, member, precision=lax.Precision.HIGHEST)
    local_count = jnp.sum(member, axis=0)
    group_total, group_count = lax.psum((local_total, local_count), "grp")
    group_mean = group_total / jnp.maximum(group_count, 1.0)
    advantage = reward - jnp.dot(member, group_mean, precision=lax.Precision.HIGHEST)
    members = jnp.dot(member, group_count, precision=lax.Precision.HIGHEST)
    weight = advantage / (members * seq_len.astype(jnp.float32))
    starts = jnp.cumsum(seq_len) - seq_len
    to_learner = targets[None, :] == jnp.arange(sources, dtype=jnp.int32)[:, None]
    slot_len = jnp.sum(jnp.where(to_learner, seq_len[None, :], 0), axis=1)
    slot_start = jnp.sum(jnp.where(to_learner, starts[None, :], 0), axis=1)
    slot_coef = jnp.sum(jnp.where(to_learner, weight[None, :], 0.0), axis=1).astype(jnp.bfloat16)
    position = jnp.arange(LMAX, dtype=jnp.int32)
    is_valid = position[None, :] < slot_len[:, None]
    token_index = jnp.where(is_valid, slot_start[:, None] + position[None, :], 0)
    send_x = jnp.where(is_valid[..., None], activations[token_index], jnp.zeros((), jnp.bfloat16))
    slot_upstream = upstream.reshape(sources, LMAX, upstream.shape[1])
    rows_x, row_coef = (
        lax.all_to_all(send_x, "grp", split_axis=0, concat_axis=0, tiled=True),
        lax.all_to_all(slot_coef, "grp", split_axis=0, concat_axis=0, tiled=True),
    )
    gathered = lax.all_gather(slot_upstream, "tp", axis=2, tiled=True)
    partial_value = row_squares(rows_x, gathered, LMAX)
    squares = lax.psum(partial_value, "tp")
    ghost_rms = jnp.sqrt(squares / (D * VW) + epsilon)
    clip_factor = clip_limit / jnp.maximum(ghost_rms, clip_limit)
    factor = row_coef.astype(jnp.float32) * clip_factor
    scaled = (gathered.astype(jnp.float32) * factor[:, None, None]).astype(jnp.bfloat16)
    local_term = lax.dot_general(
        rows_x.reshape(-1, rows_x.shape[2]),
        scaled.reshape(-1, scaled.shape[2]),
        (((0,), (0,)), ((), ())),
        preferred_element_type=jnp.float32,
    )
    gradient = lax.psum(local_term, "grp")
    return (gradient, ghost_rms[None, :])


def iota(shape, axis):
    return lax.broadcasted_iota(jnp.int32, shape, axis)


def terms(value):
    high = value.astype(jnp.bfloat16)
    rest = value - high.astype(jnp.float32)
    middle = rest.astype(jnp.bfloat16)
    low = (rest - middle.astype(jnp.float32)).astype(jnp.bfloat16)
    return high, middle, low


def mm(left, right, dims=((1,), (0,))):
    return lax.dot_general(left, right, (dims, ((), ())), preferred_element_type=jnp.float32)


NT = ((1,), (1,))
TN = ((0,), (0,))


def onehot(condition):
    return jnp.where(condition, 1.0, 0.0).astype(jnp.bfloat16)


def rows_kernel(row_max, len_ref, learner_ref, reward_ref, group_ref, x_ref, u_ref, out_ref):
    tokens = x_ref.shape[0]
    slots = u_ref.shape[0]
    rows = len_ref.shape[1]
    lane = iota((SUB, LANES), 1)
    row_of = lax.div(lane, row_max)
    place = lane - row_of * row_max
    table_len = jnp.zeros((SUB, LANES), jnp.int32)
    table_start = jnp.zeros((SUB, LANES), jnp.int32)
    table_group = jnp.zeros((SUB, LANES), jnp.int32)
    table_reward = jnp.zeros((SUB, LANES), jnp.float32)
    start = jnp.int32(0)
    for k in range(rows):
        mine = row_of == learner_ref[0, k]
        table_len = jnp.where(mine, len_ref[0, k], table_len)
        table_start = jnp.where(mine, start, table_start)
        table_group = jnp.where(mine, group_ref[0, k], table_group)
        table_reward = jnp.where(mine, reward_ref[0, k], table_reward)
        start = start + len_ref[0, k]
    source_token = jnp.where(place < table_len, table_start + place, -1)
    token_at = onehot(iota((tokens, LANES), 0) == source_token[:1])
    x = x_ref[...]
    u = u_ref[...]
    slot_x = mm(token_at, x, TN).astype(jnp.bfloat16)
    slot_u = mm(onehot(iota((LANES, slots), 0) == iota((LANES, slots), 1) + HALF), u).astype(jnp.bfloat16)
    gram = mm(slot_x, slot_x, NT) + mm(slot_u, slot_u, NT)
    across, down = iota((LANES, LANES), 1), iota((LANES, LANES), 0)
    half_across, half_down = lax.div(across, HALF), lax.div(down, HALF)
    local_across, local_down = across - half_across * HALF, down - half_down * HALF
    same = (half_across == half_down) & (lax.div(local_across, row_max) == lax.div(local_down, row_max))
    gram = jnp.where(same, gram, 0.0)
    token_across = iota((SUB, LANES), 1)
    token_across = token_across - lax.div(token_across, HALF) * HALF
    pick = onehot(lax.rem(token_across, row_max) == iota((SUB, LANES), 0))
    gram_terms = [mm(pick, term) for term in terms(gram)]
    reward_terms = [term.astype(jnp.float32) for term in terms(table_reward)]
    group_high = lax.div(table_group, 256)
    values = reward_terms + [
        v.astype(jnp.float32) for v in (group_high, table_group - group_high * 256, table_len, table_start)
    ]
    which = iota((SUB, LANES), 0)
    table = jnp.zeros((SUB, LANES), jnp.float32)
    for index, value in enumerate(values):
        table = jnp.where(which == index, value, table)
    out_ref[:slots] = u
    out_ref[slots:] = small_rows(gram_terms, table)


def small_rows(gram_terms, table):
    return jnp.concatenate(
        [
            jnp.concatenate([gram_terms[0], gram_terms[1]], axis=1),
            jnp.concatenate([gram_terms[2], table], axis=1),
        ],
        axis=0,
    ).astype(jnp.bfloat16)


def parse(rows):
    rows = rows.astype(jnp.float32)
    return rows[:SUB, :LANES], rows[:SUB, LANES:], rows[SUB:, :LANES], rows[SUB:, LANES:]


def pack_kernel(head_ref, other_ref, placed_ref, out_ref):
    slots = HALF - TILE
    mine = parse(head_ref[slots:])
    other = parse(other_ref[slots:])
    gram = (mine[0] + mine[1] + mine[2]) + (other[0] + other[1] + other[2])
    out_ref[slots:HALF] = small_rows([term.astype(jnp.float32) for term in terms(gram)], mine[3])
    out_ref[HALF : HALF + slots] = other_ref[:slots]


def place_kernel(sources, row_max, head_ref, x_ref, out_ref, spread_ref, pick_ref, expand_ref):
    tokens, features = x_ref.shape
    width = head_ref.shape[1]
    out_ref[:HALF] = head_ref[...]
    base = 2 * HALF - TILE
    for chunk in range(features // width):
        out_ref[base + chunk * tokens : base + (chunk + 1) * tokens] = x_ref[:, chunk * width : (chunk + 1) * width]
    me = lax.axis_index("grp")
    slots = sources * HALF
    lane = iota((LANES, slots), 1)
    block = lax.div(lane, HALF)
    learner = lax.bitwise_xor(block, me)
    within = lane - block * HALF
    source = lax.div(within, row_max)
    place = within - source * row_max
    used = source < sources
    local = iota((LANES, slots), 0)
    x_local = (local == learner * row_max + place) & used
    u_local = (local == within + HALF) & used
    for m in range(sources):
        origin = lax.bitwise_xor(me, m)
        spread_ref[m * LANES : (m + 1) * LANES, :slots] = onehot(x_local & (source == origin))
        spread_ref[m * LANES : (m + 1) * LANES, slots:] = onehot(u_local & (block == m))
    expand_ref[...] = onehot((local == block * sources + source) & used)
    lane = iota((slots, LANES), 0)
    block = lax.div(lane, HALF)
    source = lax.div(lane - block * HALF, row_max)
    pick_ref[...] = onehot((iota((slots, LANES), 1) == block * sources + source) & (source < sources))


def final_kernel(sources, row_max, tokens, total, *refs):
    mine = refs[:sources]
    other = refs[sources : 2 * sources]
    spread_ref, pick_ref, expand_ref = refs[2 * sources : 2 * sources + 3]
    grad_ref, ghost_ref, x_ref, u_ref, out_ref, sems = refs[2 * sources + 3 :]
    me = lax.axis_index("grp")
    my_part = lax.axis_index("tp")
    width = mine[0].shape[1]
    slots = sources * HALF
    group_rows = x_ref.shape[0] // sources
    features = grad_ref.shape[0]

    for m in range(sources):
        for chunk in range(features // width):
            base = 2 * HALF - TILE + chunk * tokens
            x_ref[m * group_rows : m * group_rows + tokens, chunk * width : (chunk + 1) * width] = mine[m][
                base : base + tokens
            ]
        x_ref[m * group_rows + tokens : (m + 1) * group_rows] = jnp.zeros(
            (group_rows - tokens, features), jnp.bfloat16
        )

    small = [parse(r[HALF - TILE : HALF]) for r in mine]
    small_other = [parse(r[HALF - TILE : HALF]) for r in other]
    stack = [jnp.concatenate([s[k] for s in small], axis=1) for k in range(4)]
    stack += [jnp.concatenate([s[k] for s in small_other], axis=1) for k in range(3)]
    stack = jnp.concatenate(stack + [stack[3]], axis=0).astype(jnp.bfloat16)
    spread = mm(stack, spread_ref[...])
    piece = [spread[k * SUB : (k + 1) * SUB] for k in range(7)]
    gram = (piece[0] + piece[1] + piece[2]) + (piece[4] + piece[5] + piece[6])
    table = piece[3][:, :slots]
    per_slot = jnp.sum(gram[:, :slots] * gram[:, slots:], axis=0, keepdims=True)

    lane = iota((1, slots), 1)
    within = lane - lax.div(lane, HALF) * HALF
    source = lax.div(within, row_max)
    place = within - source * row_max
    used = source < sources
    slot_terms = [term.astype(jnp.float32) for term in terms(per_slot)]
    row_in = jnp.concatenate(
        slot_terms + [jnp.zeros((SUB - 3, slots), jnp.float32), jnp.where(place == 0, table, 0.0)], axis=0
    ).astype(jnp.bfloat16)
    row = mm(row_in, pick_ref[...])
    ghost = jnp.sqrt((row[0:1] + row[1:2] + row[2:3]) / total + epsilon)
    clip = clip_limit / jnp.maximum(ghost, clip_limit)

    row = row[SUB:]
    reward = row[0:1] + row[1:2] + row[2:3]
    group = row[3:4] * 256.0 + row[4:5]
    length = row[5:6]
    group_column = jnp.transpose(jnp.concatenate([group] * SUB, axis=0))[:, :1]
    together = onehot(group_column == group)
    real = iota((SUB, LANES), 1) < sources * sources
    counted = jnp.concatenate([row[0:3], jnp.ones((1, LANES), jnp.float32)] * 2, axis=0)
    sums = mm(jnp.where(real, counted, 0.0).astype(jnp.bfloat16), together)
    count = jnp.maximum(sums[3:4], 1.0)
    advantage = reward - (sums[0:1] + sums[1:2] + sums[2:3]) / count
    coef = advantage / (count * jnp.maximum(length, 1.0))
    factor = coef.astype(jnp.bfloat16).astype(jnp.float32) * clip
    factor_terms = [term.astype(jnp.float32) for term in terms(factor)[:2]]
    factor = mm(jnp.concatenate(factor_terms * (SUB // 2), axis=0).astype(jnp.bfloat16), expand_ref[...])

    length, begin = table[5:6].astype(jnp.int32), table[6:7].astype(jnp.int32)
    target = jnp.where(used & (place < length), lax.bitwise_xor(source, me) * group_rows + begin + place, -1)
    chosen = iota((sources * group_rows, slots), 0) == target
    pick_high = jnp.where(chosen, factor[0:1], 0.0).astype(jnp.bfloat16)
    pick_low = jnp.where(chosen, factor[1:2], 0.0).astype(jnp.bfloat16)
    for q, (group_refs, first) in enumerate(((mine, 0), (other, 0), (mine, HALF), (other, HALF))):
        columns = jnp.concatenate([r[first : first + HALF] for r in group_refs], axis=0)
        scaled = (mm(pick_high, columns) + mm(pick_low, columns)).astype(jnp.bfloat16)
        at = pl.multiple_of(lax.bitwise_xor(my_part, q) * width, width)
        u_ref[:, pl.ds(at, width)] = scaled
    scaled = u_ref[...]
    copies = []
    for chunk in range(features // width):
        part = pl.ds(chunk * width, width)
        out_ref[part] = mm(x_ref[:, chunk * width : (chunk + 1) * width], scaled, TN)
        copies.append(pltpu.make_async_copy(out_ref.at[part], grad_ref.at[part], sems.at[chunk]))
        copies[-1].start()
    ghost_ref[...] = ghost[:, :sources]
    for copy in copies:
        copy.wait()


def swap(value, axis, mask):
    size = lax.axis_size(axis)
    return lax.ppermute(value, axis, [(i, i ^ mask) for i in range(size)])


def gathered(activations, upstream, row_lengths, learner_of, rewards, prompt_group):
    sources = lax.axis_size("grp")
    parts = lax.axis_size("tp")
    tokens, features = activations.shape
    slots, width = upstream.shape
    row_max = slots // sources
    vmem = pl.BlockSpec(memory_space=pltpu.VMEM)
    smem = pl.BlockSpec(memory_space=pltpu.SMEM)
    head = pl.pallas_call(
        functools.partial(rows_kernel, row_max),
        out_shape=jax.ShapeDtypeStruct((HALF, width), jnp.bfloat16),
        in_specs=[smem] * 4 + [vmem] * 2,
        out_specs=vmem,
        compiler_params=pltpu.CompilerParams(vmem_limit_bytes=60000 * 1024),
        name="rows",
    )(row_lengths, learner_of, rewards, prompt_group, activations, upstream)
    other_head = swap(head, "tp", 2)
    lanes = sources * HALF
    packed_shape = jax.ShapeDtypeStruct((2 * HALF - TILE + features // width * tokens, width), jnp.bfloat16)
    placed, spread, pick, expand = pl.pallas_call(
        functools.partial(place_kernel, sources, row_max),
        out_shape=(
            packed_shape,
            jax.ShapeDtypeStruct((sources * LANES, 2 * lanes), jnp.bfloat16),
            jax.ShapeDtypeStruct((lanes, LANES), jnp.bfloat16),
            jax.ShapeDtypeStruct((LANES, lanes), jnp.bfloat16),
        ),
        in_specs=[vmem, vmem],
        out_specs=(vmem, vmem, vmem, vmem),
        cost_estimate=pl.CostEstimate(flops=3_000_000, bytes_accessed=4_000_000, transcendentals=0),
        compiler_params=pltpu.CompilerParams(vmem_limit_bytes=8 * MIB),
        name="place",
    )(head, activations)
    packed = pl.pallas_call(
        pack_kernel,
        out_shape=packed_shape,
        in_specs=[vmem] * 3,
        out_specs=vmem,
        input_output_aliases={2: 0},
        compiler_params=pltpu.CompilerParams(vmem_limit_bytes=8 * MIB),
        name="pack",
    )(head, other_head, placed)
    blocks = {0: packed}
    masks = [m for m in range(sources - 2, 0, -2)]
    for m in masks:
        blocks[m] = swap(packed, "grp", m)
    for m in [0] + masks[::-1]:
        blocks[m + 1] = swap(blocks[m], "grp", 1)
    mine = [blocks[m] for m in range(sources)]
    other = [swap(b, "tp", 1) for b in mine]
    group_rows = -(-tokens // TILE) * TILE
    gradient, ghost = pl.pallas_call(
        functools.partial(final_kernel, sources, row_max, tokens, float(features * parts * width * parts)),
        out_shape=(
            jax.ShapeDtypeStruct((features, width * parts), jnp.float32),
            jax.ShapeDtypeStruct((1, sources), jnp.float32),
        ),
        in_specs=[vmem] * (2 * sources + 3),
        out_specs=(pl.BlockSpec(memory_space=pl.ANY), vmem),
        scratch_shapes=[
            pltpu.VMEM((sources * group_rows, features), jnp.bfloat16),
            pltpu.VMEM((sources * group_rows, width * parts), jnp.bfloat16),
            pltpu.VMEM((features, width * parts), jnp.float32),
            pltpu.SemaphoreType.DMA((features // width,)),
        ],
        compiler_params=pltpu.CompilerParams(vmem_limit_bytes=24 * MIB),
        name="final",
    )(*mine, *other, spread, pick, expand)
    return gradient, ghost


def power_of_two(value):
    return value & (value - 1) == 0


def local(activations, upstream, *table):
    sources = lax.axis_size("grp")
    parts = lax.axis_size("tp")
    tokens, features = activations.shape
    slots, width = upstream.shape
    fits = (
        power_of_two(sources)
        and parts == 4
        and slots == HALF - TILE
        and sources <= SUB
        and LMAX <= SUB
        and width == 2 * LANES
        and features % width == 0
        and tokens % SUB == 0
    )
    return (gathered if fits else general)(activations, upstream, *table)


def solution(mesh):
    in_specs = (
        P("grp", "tp"),
        P("grp", "tp"),
        P("grp", None),
        P("grp", None),
        P("grp", None),
        P("grp", None),
    )
    out_specs = (P("tp", None), P("grp", None))
    return jax.shard_map(local, mesh=mesh, in_specs=in_specs, out_specs=out_specs, check_vma=False)
```
